32 devices in a mesh: seq: 8 (over z, x), qblk: 4 (over y, core).
Axes of the slice: x: 2, y: 2, z: 4, core: 2. Of those that a mesh axis runs over, the one named last changes fastest.
Arguments:
- queries: bfloat16 [4096, 8192], P(('seq', 'qblk')), may hold values from -33 to 33
- key_states: bfloat16 [4096, 1024], P(('seq', 'qblk')), may hold values from -6 to 6
- value_states: bfloat16 [4096, 1024], P(('seq', 'qblk')), may hold values from -6 to 6
- block_list: int32 [64, 32, 16], replicated, may hold values from 0 to 31, as said below
- block_count: int32 [64, 32], replicated, may hold values from 1 to 16, as said below
Outputs:
- attended: bfloat16 [4096, 8192], P(('seq', 'qblk'))
The draws below stay inside these ranges and needn't reach their ends.
Inputs may be any that keep to these rules, and one draw needn't show every extreme that they name: `block_list`: for each head and query block, the first block_count entries are distinct key blocks no later than the query block, among them the query block itself; the remaining entries are 0. block_count[h, i] <= i + 1.
All inputs are finite; a program needn't handle non-finite values.
Results may differ from the reference program's by a relative error of at most 0.0044.
Values may be sent and summed in bfloat16 or wider, within the bound.
A program may use at most 64 MiB of HBM per device.

```python
import jax
import jax.numpy as jnp
from jax import lax

H = 64
KVH = 8
HEAD_SIZE = 128
BLK = 128
MAXB = 16
SEQ = 4096
NQB = 32


def list_parts(key):
    folded = jax.random.fold_in(key, 101)
    k_vert, k_rand, k_low, k_len = jax.random.split(folded, 4)
    query_ids = jnp.arange(NQB, dtype=jnp.int32)[None, :, None]
    key_ids = jnp.arange(NQB, dtype=jnp.int32)[None, None, :]
    vertical = jax.random.randint(k_vert, (H, 2, 1, 1), 0, NQB)
    priority = 1 + 8 * (key_ids == query_ids).astype(jnp.int32) + 2 * (key_ids == 0).astype(jnp.int32) + (key_ids == query_ids - 1).astype(jnp.int32) + (key_ids == vertical[:, 0]).astype(jnp.int32) + (key_ids == vertical[:, 1]).astype(jnp.int32)
    jitter = jax.random.randint(k_rand, (H, NQB, NQB), 0, 4096)
    ranking = jnp.where(key_ids <= query_ids, priority * 16777216 + jitter * 2048 + key_ids, -1 - key_ids)
    chosen = lax.top_k(ranking, MAXB)[1].astype(jnp.int32)
    floor_len = jax.random.randint(k_low, (H, 1), max(MAXB // 4, 2), MAXB + 1)
    length = jax.random.randint(k_len, (H, NQB), floor_len, MAXB + 1)
    query_col = jnp.arange(NQB, dtype=jnp.int32)[None, :]
    length = jnp.where(query_col == NQB - 1, MAXB, length)
    counts_all = jnp.minimum(length, query_col + 1).astype(jnp.int32)
    slot_ids = jnp.arange(MAXB, dtype=jnp.int32)[None, None, :]
    chosen = jnp.where(slot_ids < counts_all[:, :, None], chosen, 0).astype(jnp.int32)
    return (chosen, counts_all)


def draw_block_list(key, part):
    return list_parts(key)[0]


def draw_block_count(key, part):
    return list_parts(key)[1]


def vector_parts(key):
    folded = jax.random.fold_in(key, 202)
    k_key, k_query = jax.random.split(folded, 2)
    keys_final = jnp.clip(jax.random.normal(k_key, (SEQ, KVH * HEAD_SIZE), jnp.float32), -6.0, 6.0)
    queries_final = jnp.clip(jax.random.normal(k_query, (SEQ, H * HEAD_SIZE), jnp.float32), -6.0, 6.0)
    return (queries_final, keys_final)


def draw_queries(key, part):
    return vector_parts(key)[0].astype(jnp.bfloat16)


def draw_key_states(key, part):
    return vector_parts(key)[1].astype(jnp.bfloat16)


def block_scale(stream_key, dims, pieces, low, high):
    loudness, own = 1.0, jax.random.fold_in(stream_key, 6)
    for position, blocks in pieces:
        heights = jnp.exp(jax.random.uniform(jax.random.fold_in(own, position), (blocks,), jnp.float32, low / len(pieces), high / len(pieces)))
        loudness = loudness * jnp.repeat(heights, dims[position] // blocks).reshape([-1 if axis == position else 1 for axis in range(len(dims))])
    return loudness


def bell_draw(stream_key, extent, spread, most, cuts=(), kind=jnp.bfloat16):
    entries = spread * jax.random.normal(stream_key, extent, jnp.float32)
    if cuts:
        entries = entries * block_scale(stream_key, extent, cuts, -0.22, 0.18)
    return jnp.clip(entries, -most, most).astype(kind)


def setup_inputs(seed: int = 0) -> dict:
    streams_of = jax.random.split(jax.random.key(seed), 6)
    return {
        "queries": draw_queries(jax.random.fold_in(streams_of[5], 71), 0),
        "key_states": draw_key_states(jax.random.fold_in(streams_of[5], 71), 0),
        "value_states": bell_draw(streams_of[2], (SEQ, KVH * HEAD_SIZE), 1.0, 6.0, ((0, 32),)),
        "block_list": draw_block_list(jax.random.fold_in(streams_of[5], 71), 0),
        "block_count": draw_block_count(jax.random.fold_in(streams_of[5], 71), 0),
    }


def reference(queries, key_states, value_states, block_list, block_count):
    block_total = SEQ // BLK
    group_size = H // KVH
    score_scale = HEAD_SIZE ** -0.5
    query_grid = queries.reshape(block_total, BLK, H, HEAD_SIZE)
    kv_grid = jnp.concatenate([key_states.reshape(block_total, BLK, KVH, HEAD_SIZE), value_states.reshape(block_total, BLK, KVH, HEAD_SIZE)], axis=3)
    query_pos = jnp.arange(block_total, dtype=jnp.int32)[:, None, None, None] * BLK + jnp.arange(BLK, dtype=jnp.int32)[None, :, None, None]
    slot_ids = jnp.arange(MAXB, dtype=jnp.int32)[None, None, :, None]
    inner_pos = jnp.arange(BLK, dtype=jnp.int32)[None, None, None, :]

    def per_head(head_id):
        query_head = lax.dynamic_index_in_dim(query_grid, head_id, axis=2, keepdims=False).astype(jnp.float32)
        kv_head = lax.dynamic_index_in_dim(kv_grid, head_id // group_size, axis=2, keepdims=False)
        indices = lax.dynamic_index_in_dim(block_list, head_id, axis=0, keepdims=False).astype(jnp.int32)
        counts_now = lax.dynamic_index_in_dim(block_count, head_id, axis=0, keepdims=False).astype(jnp.int32)
        key_value_tiles = kv_head[indices]
        attention_scores = jnp.einsum("psi,pcai->psca", query_head, key_value_tiles[..., :HEAD_SIZE].astype(jnp.float32)) * score_scale
        key_pos = indices[:, None, :, None] * BLK + inner_pos
        usable = (slot_ids < counts_now[:, None, None, None]) & (key_pos <= query_pos)
        attention_scores = jnp.where(usable, attention_scores, -jnp.inf)
        highest = jnp.max(attention_scores, axis=(2, 3), keepdims=True)
        weights = jnp.exp(attention_scores - highest)
        weight_sum = jnp.sum(weights, axis=(2, 3))
        rounded_length = lax.optimization_barrier(weights.astype(jnp.bfloat16)).astype(jnp.float32)
        combined_output = jnp.einsum("hoac,hact->hot", rounded_length, key_value_tiles[..., HEAD_SIZE:].astype(jnp.float32))
        return (combined_output / weight_sum[:, :, None]).astype(jnp.bfloat16)

    per_block = lax.map(per_head, jnp.arange(H, dtype=jnp.int32))
    return per_block.transpose(1, 2, 0, 3).reshape(SEQ, H * HEAD_SIZE)
```

```python
import functools

import jax
import jax.numpy as jnp
from jax import lax
from jax.experimental import pallas as pl
from jax.experimental.pallas import tpu as pltpu
from jax.sharding import Mesh, PartitionSpec as P

H = 64
KVH = 8
D = 128
BLK = 128
MAXB = 16
GROUP = H // KVH
TEAM = 4
STAGES = KVH // TEAM
PAIRS = GROUP // 2
COLS = GROUP * D
LOG2E = 1.4426950408889634
C = D ** (-0.5) * LOG2E
CHUNK = 2
MESH = pl.DeviceIdType.MESH


def over_rows(x, op):
    n = x.shape[0] // 8
    x = x.reshape(n, 8, x.shape[1])
    while n > 1:
        n //= 2
        x = op(x[:n], x[n:])
    return x[0]


def score_steps(queries, key_at, bias, tri, s_ref, tops):
    zero = jnp.zeros((BLK, D), jnp.bfloat16)
    w = jnp.concatenate(
        [
            jnp.concatenate([queries[:, :D], zero], axis=1),
            jnp.concatenate([zero, queries[:, D:]], axis=1),
        ],
        axis=0,
    )
    for first in range(0, MAXB, CHUNK):
        slots = range(first, first + CHUNK)
        keys = jnp.concatenate(
            [jnp.concatenate([key_at(0, m), key_at(1, m)], axis=1) for m in slots], axis=0
        )
        s = lax.dot_general(keys, w, (((1,), (1,)), ((), ())), preferred_element_type=jnp.float32)
        for m in slots:
            for n in range(2):
                part = s[(m - first) * BLK : (m - first + 1) * BLK, n * BLK : (n + 1) * BLK]
                if m == 0:
                    part = jnp.where(tri, part, -jnp.inf)
                s_ref[n, m * BLK : (m + 1) * BLK, :] = part
                top = over_rows(part, jnp.maximum)
                if m > 0:
                    top = top + bias(n, m)
                tops[n] = top if tops[n] is None else jnp.maximum(tops[n], top)
        yield


def weight_steps(tops, value_at, bias, s_ref, results):
    highest = [
        jnp.broadcast_to(jnp.max(t, axis=0, keepdims=True) * C, (8, BLK)) for t in tops
    ]
    total = [None, None]
    acc = [None, None]
    for first in range(0, MAXB, CHUNK):
        slots = range(first, first + CHUNK)
        for n in range(2):
            parts = []
            for m in slots:
                shift = highest[n] if m == 0 else highest[n] - bias(n, m)
                s = s_ref[n, m * BLK : (m + 1) * BLK, :].reshape(BLK // 8, 8, BLK)
                p = jnp.exp2(s * C - shift[None]).reshape(BLK, BLK)
                t = over_rows(p, jnp.add)
                total[n] = t if total[n] is None else total[n] + t
                parts.append(p.astype(jnp.bfloat16))
            values = jnp.concatenate([value_at(n, m) for m in slots], axis=1)
            o = jnp.dot(values, jnp.concatenate(parts, axis=0), preferred_element_type=jnp.float32)
            acc[n] = o if acc[n] is None else acc[n] + o
        yield
    for n in range(2):
        scale = 1.0 / jnp.sum(total[n], axis=0, keepdims=True)
        results.append((acc[n] * scale).T.astype(jnp.bfloat16))


def interleave(*steps):
    steps = list(steps)
    while steps:
        for one in list(steps):
            try:
                next(one)
            except StopIteration:
                steps.remove(one)


def kernel(
    ng, ny, q_ref, k_ref, v_ref, list_ref, count_ref, out_ref,
    buf_a, buf_b, own_kv, q_buf, o_buf, s_ref, lists, counts,
    list_sem, q_own, o_own, kv_own,
    plane_send, q_send, q_recv, o_send, o_recv,
    up_send, up_recv, side_send, side_recv,
):
    bufs = (buf_a, buf_b)
    c = lax.axis_index("core")
    chip = lax.axis_index("seq") * ny + lax.axis_index("y")
    g = chip // TEAM
    j = chip % TEAM
    last = ng - 1

    def at_chip(t):
        return {"seq": t // ny, "y": t % ny}

    def mate(k):
        return (j + k) % TEAM

    side = {"core": 1 - c}
    above = at_chip(jnp.minimum(chip + TEAM, ng * TEAM - 1))
    below = at_chip(jnp.maximum(chip - TEAM, 0))

    copies = [
        pltpu.make_async_copy(
            list_ref.at[pl.ds(j * 2 * GROUP, 2 * GROUP), pl.ds(pl.multiple_of(g * 8, 8), 8), :],
            lists, list_sem.at[0],
        ),
        pltpu.make_async_copy(
            count_ref.at[pl.ds(pl.multiple_of(j * 2 * GROUP, 2 * GROUP), 2 * GROUP), :],
            counts, list_sem.at[1],
        ),
    ]
    for copy in copies:
        copy.start()

    barrier = pltpu.get_barrier_semaphore()
    for k in range(1, TEAM):
        pl.semaphore_signal(
            barrier, inc=1, device_id=at_chip(g * TEAM + mate(k)), device_id_type=MESH
        )
    pl.semaphore_signal(barrier, inc=1, device_id=side, device_id_type=MESH)

    @pl.when(g < last)
    def _():
        pl.semaphore_signal(barrier, inc=1, device_id=above, device_id_type=MESH)

    @pl.when(g > 0)
    def _():
        pl.semaphore_signal(barrier, inc=1, device_id=below, device_id_type=MESH)

    for h in range(KVH):
        own_kv[h, 0] = k_ref[:, h * D : (h + 1) * D]
        own_kv[h, 1] = v_ref[:, h * D : (h + 1) * D].T

    own_q = []
    for s in range(STAGES):
        copy = pltpu.make_async_copy(
            q_ref.at[:, pl.ds(pl.multiple_of((j * STAGES + s) * COLS, COLS), COLS)],
            q_buf.at[s, j], q_own.at[s],
        )
        copy.start()
        own_q.append(copy)
    for s in range(STAGES):
        copy = pltpu.make_async_copy(own_kv.at[j * STAGES + s], bufs[s].at[c, g, j], kv_own.at[s])
        copy.start()
        copy.wait()

    neighbours = 4 + (g < last).astype(jnp.int32) + (g > 0).astype(jnp.int32)
    pl.semaphore_wait(barrier, neighbours)

    def plane_copy(s, k):
        to = mate(k)
        return pltpu.make_async_remote_copy(
            src_ref=own_kv.at[to * STAGES + s],
            dst_ref=bufs[s].at[c, g, j],
            send_sem=plane_send.at[s, k],
            recv_sem=up_recv.at[s, g, j],
            device_id=at_chip(g * TEAM + to),
            device_id_type=MESH,
        )

    def q_copy(s, k):
        to = mate(k)
        return pltpu.make_async_remote_copy(
            src_ref=q_ref.at[:, pl.ds(pl.multiple_of((to * STAGES + s) * COLS, COLS), COLS)],
            dst_ref=q_buf.at[s, j],
            send_sem=q_send.at[s, k],
            recv_sem=q_recv.at[s, j],
            device_id=at_chip(g * TEAM + to),
            device_id_type=MESH,
        )

    def q_arrival(s, k):
        frm = mate(k)
        return pltpu.make_async_remote_copy(
            src_ref=q_buf.at[s, frm],
            dst_ref=q_buf.at[s, frm],
            send_sem=q_send.at[s, k],
            recv_sem=q_recv.at[s, frm],
            device_id=at_chip(g * TEAM + frm),
            device_id_type=MESH,
        )

    def up_copy(s, group, member):
        piece = bufs[s].at[c, group, member]
        return pltpu.make_async_remote_copy(
            src_ref=piece, dst_ref=piece,
            send_sem=up_send.at[s, group, member],
            recv_sem=up_recv.at[s, group, member],
            device_id=above,
            device_id_type=MESH,
        )

    def side_copy(s, core, group, member):
        piece = bufs[s].at[core, group, member]
        return pltpu.make_async_remote_copy(
            src_ref=piece, dst_ref=piece,
            send_sem=side_send.at[s, group, member],
            recv_sem=side_recv.at[s, group, member],
            device_id=side,
            device_id_type=MESH,
        )

    def pass_on(s, group, member):
        pl.when(g < last)(up_copy(s, group, member).start)
        side_copy(s, c, group, member).start()

    def take(s, group, member):
        up_copy(s, group, member).wait_recv()
        pass_on(s, group, member)

    def take_group(s, group):
        def step(i, _):
            take(s, group, i)
            return 0

        lax.fori_loop(0, TEAM, step, 0)

    def take_below(s, low, high):
        def step(t, _):
            take(s, g - 1 - t // TEAM, t % TEAM)
            return 0

        lax.fori_loop(jnp.minimum(g, low) * TEAM, jnp.minimum(g, high) * TEAM, step, 0)

    def wait_sides(s):
        def step(t, _):
            side_copy(s, 1 - c, t // TEAM, t % TEAM).wait_recv()
            return 0

        lax.fori_loop(0, (g + 1) * TEAM, step, 0)

    for s in range(STAGES):
        for k in range(1, TEAM):
            plane_copy(s, k).start()
    pass_on(0, g, j)
    for k in range(1, TEAM):
        q_copy(0, k).start()
    for k in range(1, TEAM):
        take(0, g, mate(k))
    take_below(0, 0, ng)
    for k in range(1, TEAM):
        q_copy(1, k).start()
    pass_on(1, g, j)
    for k in range(1, TEAM):
        take(1, g, mate(k))
    wait_sides(0)
    for copy in copies:
        copy.wait()

    tri = lax.broadcasted_iota(jnp.int32, (BLK, BLK), 0) <= lax.broadcasted_iota(
        jnp.int32, (BLK, BLK), 1
    )

    def wait_queries(s):
        own_q[s].wait()
        for k in range(1, TEAM):
            q_arrival(s, k).wait_recv()

    def pair_of(s, t):
        member = mate(1 + t // PAIRS)
        pair = t % PAIRS
        row = 2 * member + c
        block = g * 8 + row
        slots = []
        limits = []
        for n in range(2):
            head = s * GROUP + pair * 2 + n
            first = lists[head, row, 0]
            listed = [block]
            for m in range(1, MAXB):
                entry = lists[head, row, m]
                listed.append(jnp.where(entry == block, first, entry))
            slots.append([e.astype(jnp.uint32) for e in listed])
            limits.append(counts[head, block])

        def bias(n, m):
            return jnp.where(m < limits[n], 0.0, -jnp.inf).astype(jnp.float32)

        def piece(n, m, which):
            e = slots[n][m]
            return bufs[s][e % 2, e // 8, (e // 2) % TEAM, which]

        return member, pair, bias, piece

    def scores(s, t, side_ref, tops):
        member, pair, bias, piece = pair_of(s, t)
        queries = q_buf[s, member, :, pl.ds(pl.multiple_of(pair * 2 * D, 2 * D), 2 * D)]
        return score_steps(queries, lambda n, m: piece(n, m, 0), bias, tri, side_ref, tops)

    def weights(s, t, side_ref, tops, results):
        _, _, bias, piece = pair_of(s, t)
        return weight_steps(tops, lambda n, m: piece(n, m, 1), bias, side_ref, results)

    def out_local(s, pair):
        mine = pl.multiple_of(pair * 2 * D, 2 * D)
        cols = pl.multiple_of((j * STAGES + s) * COLS + pair * 2 * D, 2 * D)
        return pltpu.make_async_copy(
            o_buf.at[s, j, :, pl.ds(mine, 2 * D)], out_ref.at[:, pl.ds(cols, 2 * D)],
            o_own.at[s, pair],
        )

    def out_copy(s, member, pair, owner):
        mine = pl.multiple_of(pair * 2 * D, 2 * D)
        cols = pl.multiple_of((owner * STAGES + s) * COLS + pair * 2 * D, 2 * D)
        return pltpu.make_async_remote_copy(
            src_ref=o_buf.at[s, member, :, pl.ds(mine, 2 * D)],
            dst_ref=out_ref.at[:, pl.ds(cols, 2 * D)],
            send_sem=o_send.at[s, member, pair],
            recv_sem=o_recv.at[s, owner, pair],
            device_id=at_chip(g * TEAM + member),
            device_id_type=MESH,
        )

    def emit(s, t, results):
        member = mate(1 + t // PAIRS)
        pair = t % PAIRS
        o_buf[s, member, :, pl.ds(pl.multiple_of(pair * 2 * D, 2 * D), 2 * D)] = jnp.concatenate(
            results, axis=1
        )
        pl.when(member != j)(out_copy(s, member, pair, j).start)
        pl.when(member == j)(out_local(s, pair).start)

    total = TEAM * PAIRS

    def begin(s):
        tops = [None, None]
        interleave(scores(s, 0, s_ref.at[0], tops))
        return tuple(tops)

    def attend(s, low, high, tops):
        def step(i, tops):
            for half in range(2):
                t = 2 * i + half
                later = [None, None]
                results = []
                interleave(
                    scores(s, jnp.minimum(t + 1, total - 1), s_ref.at[1 - half], later),
                    weights(s, t, s_ref.at[half], list(tops), results),
                )
                emit(s, t, results)
                tops = tuple(later)
            return tops

        return lax.fori_loop(low, high, step, tops)

    half = total // 2
    wait_queries(0)
    tops = begin(0)
    tops = attend(0, 0, half // 4, tops)
    take_below(1, 0, 1)
    tops = attend(0, half // 4, half // 2, tops)
    take_below(1, 1, 2)
    tops = attend(0, half // 2, 3 * half // 4, tops)
    take_below(1, 2, ng)
    attend(0, 3 * half // 4, half, tops)
    wait_sides(1)
    wait_queries(1)
    attend(1, 0, half, begin(1))

    for s in range(STAGES):
        for k in range(1, TEAM):
            plane_copy(s, k).wait_send()
            q_copy(s, k).wait_send()
            for pair in range(PAIRS):
                out_copy(s, mate(k), pair, j).wait_send()
                out_copy(s, j, pair, mate(k)).wait_recv()
        for pair in range(PAIRS):
            out_local(s, pair).wait()

        def step(t, _):
            pl.when(g < last)(up_copy(s, t // TEAM, t % TEAM).wait_send)
            side_copy(s, c, t // TEAM, t % TEAM).wait_send()
            return 0

        lax.fori_loop(0, (g + 1) * TEAM, step, 0)


def fused(ng, ny, q, k, v, block_list, block_count):
    vmem = pl.BlockSpec(memory_space=pltpu.VMEM)
    anywhere = pl.BlockSpec(memory_space=pl.ANY)
    buf = pltpu.VMEM((2, ng, TEAM, 2, BLK, D), jnp.bfloat16)
    dma = pltpu.SemaphoreType.DMA
    return pl.pallas_call(
        functools.partial(kernel, ng, ny),
        in_specs=[anywhere, vmem, vmem, anywhere, anywhere],
        out_specs=anywhere,
        out_shape=jax.ShapeDtypeStruct(q.shape, jnp.bfloat16),
        scratch_shapes=[
            buf,
            buf,
            pltpu.VMEM((KVH, 2, BLK, D), jnp.bfloat16),
            pltpu.VMEM((STAGES, TEAM, BLK, COLS), jnp.bfloat16),
            pltpu.VMEM((STAGES, TEAM, BLK, COLS), jnp.bfloat16),
            pltpu.VMEM((2, 2, MAXB * BLK, BLK), jnp.float32),
            pltpu.SMEM((2 * GROUP, 8, MAXB), jnp.int32),
            pltpu.SMEM((2 * GROUP, block_count.shape[1]), jnp.int32),
            dma((2,)),
            dma((STAGES,)),
            dma((STAGES, PAIRS)),
            dma((STAGES,)),
            dma((STAGES, TEAM)),
            dma((STAGES, TEAM)),
            dma((STAGES, TEAM)),
            dma((STAGES, TEAM, PAIRS)),
            dma((STAGES, TEAM, PAIRS)),
            dma((STAGES, ng, TEAM)),
            dma((STAGES, ng, TEAM)),
            dma((STAGES, ng, TEAM)),
            dma((STAGES, ng, TEAM)),
        ],
        compiler_params=pltpu.CompilerParams(
            collective_id=0, has_side_effects=True, vmem_limit_bytes=48 * 1024 * 1024
        ),
        name="heads_attend",
    )(q, k, v, block_list, block_count)


def shards(q, k, v, block_list, block_count):
    ny = lax.axis_size("y")
    ng = lax.axis_size("seq") * ny // TEAM
    return fused(ng, ny, q, k, v, block_list, block_count)


def solution(mesh):
    n_seq, n_qblk = mesh.devices.shape
    fine = Mesh(mesh.devices.reshape(n_seq, n_qblk // 2, 2), ("seq", "y", "core"))
    rows = P(("seq", "y", "core"), None)
    return jax.shard_map(
        shards,
        mesh=fine,
        in_specs=(rows, rows, rows, P(), P()),
        out_specs=rows,
        check_vma=False,
    )
```

```python
import functools

import jax
import jax.numpy as jnp
from jax import lax
from jax.experimental import pallas as pl
from jax.experimental.pallas import tpu as pltpu
from jax.sharding import Mesh, PartitionSpec as P

H = 64
KVH = 8
D = 128
BLK = 128
MAXB = 16
GROUP = H // KVH
TEAM = 4
STAGES = KVH // TEAM
PAIRS = GROUP // 2
COLS = GROUP * D
LOG2E = 1.4426950408889634
C = D ** (-0.5) * LOG2E
CHUNK = 2
MESH = pl.DeviceIdType.MESH


def over_rows(x, op):
    n = x.shape[0] // 8
    x = x.reshape(n, 8, x.shape[1])
    while n > 1:
        n //= 2
        x = op(x[:n], x[n:])
    return x[0]


def score_steps(queries, key_at, bias, tri, s_ref, tops):
    zero = jnp.zeros((BLK, D), jnp.bfloat16)
    w = jnp.concatenate(
        [
            jnp.concatenate([queries[:, :D], zero], axis=1),
            jnp.concatenate([zero, queries[:, D:]], axis=1),
        ],
        axis=0,
    )
    for first in range(0, MAXB, CHUNK):
        slots = range(first, first + CHUNK)
        keys = jnp.concatenate(
            [jnp.concatenate([key_at(0, m), key_at(1, m)], axis=1) for m in slots], axis=0
        )
        s = lax.dot_general(keys, w, (((1,), (1,)), ((), ())), preferred_element_type=jnp.float32)
        for m in slots:
            for n in range(2):
                part = s[(m - first) * BLK : (m - first + 1) * BLK, n * BLK : (n + 1) * BLK]
                if m == 0:
                    part = jnp.where(tri, part, -jnp.inf)
                s_ref[n, m * BLK : (m + 1) * BLK, :] = part
                top = over_rows(part, jnp.maximum)
                if m > 0:
                    top = top + bias(n, m)
                tops[n] = top if tops[n] is None else jnp.maximum(tops[n], top)
        yield


def weight_steps(tops, value_at, bias, s_ref, results):
    highest = [
        jnp.broadcast_to(jnp.max(t, axis=0, keepdims=True) * C, (8, BLK)) for t in tops
    ]
    total = [None, None]
    acc = [None, None]
    for first in range(0, MAXB, CHUNK):
        slots = range(first, first + CHUNK)
        for n in range(2):
            parts = []
            for m in slots:
                shift = highest[n] if m == 0 else highest[n] - bias(n, m)
                s = s_ref[n, m * BLK : (m + 1) * BLK, :].reshape(BLK // 8, 8, BLK)
                p = jnp.exp2(s * C - shift[None]).reshape(BLK, BLK)
                t = over_rows(p, jnp.add)
                total[n] = t if total[n] is None else total[n] + t
                parts.append(p.astype(jnp.bfloat16))
            values = jnp.concatenate([value_at(n, m) for m in slots], axis=1)
            o = jnp.dot(values, jnp.concatenate(parts, axis=0), preferred_element_type=jnp.float32)
            acc[n] = o if acc[n] is None else acc[n] + o
        yield
    for n in range(2):
        scale = 1.0 / jnp.sum(total[n], axis=0, keepdims=True)
        results.append((acc[n] * scale).T.astype(jnp.bfloat16))


def interleave(*steps):
    steps = list(steps)
    while steps:
        for one in list(steps):
            try:
                next(one)
            except StopIteration:
                steps.remove(one)


def kernel(
    ng, ny, q_ref, k_ref, v_ref, list_ref, count_ref, out_ref,
    buf_a, buf_b, own_kv, q_buf, o_buf, s_ref, k_buf, v_buf, lists, counts,
    kv_load, list_sem, q_own, o_own, kv_own,
    plane_send, q_send, q_recv, o_send, o_recv,
    up_send, up_recv, side_send, side_recv,
):
    bufs = (buf_a, buf_b)
    c = lax.axis_index("core")
    chip = lax.axis_index("seq") * ny + lax.axis_index("y")
    g = chip // TEAM
    j = chip % TEAM
    last = ng - 1

    def at_chip(t):
        return {"seq": t // ny, "y": t % ny}

    def mate(k):
        return (j + k) % TEAM

    side = {"core": 1 - c}
    above = at_chip(jnp.minimum(chip + TEAM, ng * TEAM - 1))
    below = at_chip(jnp.maximum(chip - TEAM, 0))

    copies = [
        pltpu.make_async_copy(
            list_ref.at[pl.ds(pl.multiple_of(g * 8, 8), 8)], lists, list_sem.at[0]
        ),
        pltpu.make_async_copy(
            count_ref.at[pl.ds(pl.multiple_of(g * 8, 8), 8)], counts, list_sem.at[1]
        ),
    ]
    loads = [
        pltpu.make_async_copy(k_ref, k_buf, kv_load.at[0]),
        pltpu.make_async_copy(v_ref, v_buf, kv_load.at[1]),
    ]
    for copy in loads + copies:
        copy.start()

    barrier = pltpu.get_barrier_semaphore()
    for k in range(1, TEAM):
        pl.semaphore_signal(
            barrier, inc=1, device_id=at_chip(g * TEAM + mate(k)), device_id_type=MESH
        )
    pl.semaphore_signal(barrier, inc=1, device_id=side, device_id_type=MESH)

    @pl.when(g < last)
    def _():
        pl.semaphore_signal(barrier, inc=1, device_id=above, device_id_type=MESH)

    @pl.when(g > 0)
    def _():
        pl.semaphore_signal(barrier, inc=1, device_id=below, device_id_type=MESH)

    own_q = []
    for s in range(STAGES):
        copy = pltpu.make_async_copy(
            q_ref.at[:, pl.ds(pl.multiple_of((j * STAGES + s) * COLS, COLS), COLS)],
            q_buf.at[s, j], q_own.at[s],
        )
        copy.start()
        own_q.append(copy)
    for copy in loads:
        copy.wait()
    for h in range(KVH):
        own_kv[h, 0] = k_buf[:, h * D : (h + 1) * D]
        own_kv[h, 1] = v_buf[:, h * D : (h + 1) * D].T
    for s in range(STAGES):
        copy = pltpu.make_async_copy(own_kv.at[j * STAGES + s], bufs[s].at[c, g, j], kv_own.at[s])
        copy.start()
        copy.wait()

    neighbours = 4 + (g < last).astype(jnp.int32) + (g > 0).astype(jnp.int32)
    pl.semaphore_wait(barrier, neighbours)

    def plane_copy(s, k):
        to = mate(k)
        return pltpu.make_async_remote_copy(
            src_ref=own_kv.at[to * STAGES + s],
            dst_ref=bufs[s].at[c, g, j],
            send_sem=plane_send.at[s, k],
            recv_sem=up_recv.at[s, g, j],
            device_id=at_chip(g * TEAM + to),
            device_id_type=MESH,
        )

    def q_copy(s, k):
        to = mate(k)
        return pltpu.make_async_remote_copy(
            src_ref=q_ref.at[:, pl.ds(pl.multiple_of((to * STAGES + s) * COLS, COLS), COLS)],
            dst_ref=q_buf.at[s, j],
            send_sem=q_send.at[s, k],
            recv_sem=q_recv.at[s, j],
            device_id=at_chip(g * TEAM + to),
            device_id_type=MESH,
        )

    def q_arrival(s, k):
        frm = mate(k)
        return pltpu.make_async_remote_copy(
            src_ref=q_buf.at[s, frm],
            dst_ref=q_buf.at[s, frm],
            send_sem=q_send.at[s, k],
            recv_sem=q_recv.at[s, frm],
            device_id=at_chip(g * TEAM + frm),
            device_id_type=MESH,
        )

    def up_copy(s, group, member):
        piece = bufs[s].at[c, group, member]
        return pltpu.make_async_remote_copy(
            src_ref=piece, dst_ref=piece,
            send_sem=up_send.at[s, group, member],
            recv_sem=up_recv.at[s, group, member],
            device_id=above,
            device_id_type=MESH,
        )

    def side_copy(s, core, group, member):
        piece = bufs[s].at[core, group, member]
        return pltpu.make_async_remote_copy(
            src_ref=piece, dst_ref=piece,
            send_sem=side_send.at[s, group, member],
            recv_sem=side_recv.at[s, group, member],
            device_id=side,
            device_id_type=MESH,
        )

    def pass_on(s, group, member):
        pl.when(g < last)(up_copy(s, group, member).start)
        side_copy(s, c, group, member).start()

    def take(s, group, member):
        up_copy(s, group, member).wait_recv()
        pass_on(s, group, member)

    def take_group(s, group):
        def step(i, _):
            take(s, group, i)
            return 0

        lax.fori_loop(0, TEAM, step, 0)

    def take_below(s, low, high):
        def step(t, _):
            take(s, g - 1 - t // TEAM, t % TEAM)
            return 0

        lax.fori_loop(jnp.minimum(g, low) * TEAM, jnp.minimum(g, high) * TEAM, step, 0)

    def wait_sides(s):
        def step(t, _):
            side_copy(s, 1 - c, t // TEAM, t % TEAM).wait_recv()
            return 0

        lax.fori_loop(0, (g + 1) * TEAM, step, 0)

    for s in range(STAGES):
        for k in range(1, TEAM):
            plane_copy(s, k).start()
    pass_on(0, g, j)
    for k in range(1, TEAM):
        q_copy(0, k).start()
    for k in range(1, TEAM):
        take(0, g, mate(k))
    take_below(0, 0, ng)
    for k in range(1, TEAM):
        q_copy(1, k).start()
    pass_on(1, g, j)
    for k in range(1, TEAM):
        take(1, g, mate(k))
    wait_sides(0)
    for copy in copies:
        copy.wait()

    tri = lax.broadcasted_iota(jnp.int32, (BLK, BLK), 0) <= lax.broadcasted_iota(
        jnp.int32, (BLK, BLK), 1
    )

    def wait_queries(s):
        own_q[s].wait()
        for k in range(1, TEAM):
            q_arrival(s, k).wait_recv()

    def pair_of(s, t):
        member = mate(1 + t // PAIRS)
        pair = t % PAIRS
        row = 2 * member + c
        block = g * 8 + row
        slots = []
        limits = []
        for n in range(2):
            head = (j * STAGES + s) * GROUP + pair * 2 + n
            first = lists[row, 0, head]
            listed = [block]
            for m in range(1, MAXB):
                entry = lists[row, m, head]
                listed.append(jnp.where(entry == block, first, entry))
            slots.append([e.astype(jnp.uint32) for e in listed])
            limits.append(counts[row, head])

        def bias(n, m):
            return jnp.where(m < limits[n], 0.0, -jnp.inf).astype(jnp.float32)

        def piece(n, m, which):
            e = slots[n][m]
            return bufs[s][e % 2, e // 8, (e // 2) % TEAM, which]

        return member, pair, bias, piece

    def scores(s, t, side_ref, tops):
        member, pair, bias, piece = pair_of(s, t)
        queries = q_buf[s, member, :, pl.ds(pl.multiple_of(pair * 2 * D, 2 * D), 2 * D)]
        return score_steps(queries, lambda n, m: piece(n, m, 0), bias, tri, side_ref, tops)

    def weights(s, t, side_ref, tops, results):
        _, _, bias, piece = pair_of(s, t)
        return weight_steps(tops, lambda n, m: piece(n, m, 1), bias, side_ref, results)

    def out_local(s, pair):
        mine = pl.multiple_of(pair * 2 * D, 2 * D)
        cols = pl.multiple_of((j * STAGES + s) * COLS + pair * 2 * D, 2 * D)
        return pltpu.make_async_copy(
            o_buf.at[s, j, :, pl.ds(mine, 2 * D)], out_ref.at[:, pl.ds(cols, 2 * D)],
            o_own.at[s, pair],
        )

    def out_copy(s, member, pair, owner):
        mine = pl.multiple_of(pair * 2 * D, 2 * D)
        cols = pl.multiple_of((owner * STAGES + s) * COLS + pair * 2 * D, 2 * D)
        return pltpu.make_async_remote_copy(
            src_ref=o_buf.at[s, member, :, pl.ds(mine, 2 * D)],
            dst_ref=out_ref.at[:, pl.ds(cols, 2 * D)],
            send_sem=o_send.at[s, member, pair],
            recv_sem=o_recv.at[s, owner, pair],
            device_id=at_chip(g * TEAM + member),
            device_id_type=MESH,
        )

    def emit(s, t, results):
        member = mate(1 + t // PAIRS)
        pair = t % PAIRS
        o_buf[s, member, :, pl.ds(pl.multiple_of(pair * 2 * D, 2 * D), 2 * D)] = jnp.concatenate(
            results, axis=1
        )
        pl.when(member != j)(out_copy(s, member, pair, j).start)
        pl.when(member == j)(out_local(s, pair).start)

    total = TEAM * PAIRS

    def begin(s):
        tops = [None, None]
        interleave(scores(s, 0, s_ref.at[0], tops))
        return tuple(tops)

    def attend(s, low, high, tops):
        def step(i, tops):
            for half in range(2):
                t = 2 * i + half
                later = [None, None]
                results = []
                interleave(
                    scores(s, jnp.minimum(t + 1, total - 1), s_ref.at[1 - half], later),
                    weights(s, t, s_ref.at[half], list(tops), results),
                )
                emit(s, t, results)
                tops = tuple(later)
            return tops

        return lax.fori_loop(low, high, step, tops)

    half = total // 2
    wait_queries(0)
    tops = begin(0)
    tops = attend(0, 0, half // 4, tops)
    take_below(1, 0, 1)
    tops = attend(0, half // 4, half // 2, tops)
    take_below(1, 1, 2)
    tops = attend(0, half // 2, 3 * half // 4, tops)
    take_below(1, 2, ng)
    attend(0, 3 * half // 4, half, tops)
    wait_sides(1)
    wait_queries(1)
    attend(1, 0, half, begin(1))

    for s in range(STAGES):
        for k in range(1, TEAM):
            plane_copy(s, k).wait_send()
            q_copy(s, k).wait_send()
            for pair in range(PAIRS):
                out_copy(s, mate(k), pair, j).wait_send()
                out_copy(s, j, pair, mate(k)).wait_recv()
        for pair in range(PAIRS):
            out_local(s, pair).wait()

        def step(t, _):
            pl.when(g < last)(up_copy(s, t // TEAM, t % TEAM).wait_send)
            side_copy(s, c, t // TEAM, t % TEAM).wait_send()
            return 0

        lax.fori_loop(0, (g + 1) * TEAM, step, 0)


def fused(ng, ny, q, k, v, block_list, block_count):
    anywhere = pl.BlockSpec(memory_space=pl.ANY)
    buf = pltpu.VMEM((2, ng, TEAM, 2, BLK, D), jnp.bfloat16)
    dma = pltpu.SemaphoreType.DMA
    return pl.pallas_call(
        functools.partial(kernel, ng, ny),
        in_specs=[anywhere] * 5,
        out_specs=anywhere,
        out_shape=jax.ShapeDtypeStruct(q.shape, jnp.bfloat16),
        scratch_shapes=[
            buf,
            buf,
            pltpu.VMEM((KVH, 2, BLK, D), jnp.bfloat16),
            pltpu.VMEM((STAGES, TEAM, BLK, COLS), jnp.bfloat16),
            pltpu.VMEM((STAGES, TEAM, BLK, COLS), jnp.bfloat16),
            pltpu.VMEM((2, 2, MAXB * BLK, BLK), jnp.float32),
            pltpu.VMEM((BLK, KVH * D), jnp.bfloat16),
            pltpu.VMEM((BLK, KVH * D), jnp.bfloat16),
            pltpu.SMEM((2 * TEAM, MAXB, H), jnp.int32),
            pltpu.SMEM((2 * TEAM, H), jnp.int32),
            dma((2,)),
            dma((2,)),
            dma((STAGES,)),
            dma((STAGES, PAIRS)),
            dma((STAGES,)),
            dma((STAGES, TEAM)),
            dma((STAGES, TEAM)),
            dma((STAGES, TEAM)),
            dma((STAGES, TEAM, PAIRS)),
            dma((STAGES, TEAM, PAIRS)),
            dma((STAGES, ng, TEAM)),
            dma((STAGES, ng, TEAM)),
            dma((STAGES, ng, TEAM)),
            dma((STAGES, ng, TEAM)),
        ],
        compiler_params=pltpu.CompilerParams(
            collective_id=0, has_side_effects=True, vmem_limit_bytes=48 * 1024 * 1024
        ),
        name="heads_attend",
    )(*(pltpu.with_memory_space_constraint(x, pltpu.HBM) for x in (q, k, v, block_list, block_count)))


def shards(q, k, v, block_list, block_count):
    ny = lax.axis_size("y")
    ng = lax.axis_size("seq") * ny // TEAM
    return fused(ng, ny, q, k, v, block_list.transpose(1, 2, 0), block_count.T)


def solution(mesh):
    n_seq, n_qblk = mesh.devices.shape
    fine = Mesh(mesh.devices.reshape(n_seq, n_qblk // 2, 2), ("seq", "y", "core"))
    rows = P(("seq", "y", "core"), None)
    return jax.shard_map(
        shards,
        mesh=fine,
        in_specs=(rows, rows, rows, P(), P()),
        out_specs=rows,
        check_vma=False,
    )
```

```python
import functools

import jax
import jax.numpy as jnp
from jax import lax
from jax.experimental import pallas as pl
from jax.experimental.pallas import tpu as pltpu
from jax.sharding import Mesh, PartitionSpec as P

H = 64
KVH = 8
D = 128
BLK = 128
MAXB = 16
GROUP = H // KVH
TEAM = 4
STAGES = KVH // TEAM
PAIRS = GROUP // 2
PARTS = PAIRS // 2
COLS = GROUP * D
LOG2E = 1.4426950408889634
C = D ** (-0.5) * LOG2E
CHUNK = 2
MESH = pl.DeviceIdType.MESH


def over_rows(x, op):
    n = x.shape[0] // 8
    x = x.reshape(n, 8, x.shape[1])
    while n > 1:
        n //= 2
        x = op(x[:n], x[n:])
    return x[0]


def score_steps(queries, key_at, bias, tri, s_ref, tops):
    zero = jnp.zeros((BLK, D), jnp.bfloat16)
    w = jnp.concatenate(
        [
            jnp.concatenate([queries[:, :D], zero], axis=1),
            jnp.concatenate([zero, queries[:, D:]], axis=1),
        ],
        axis=0,
    )
    for first in range(0, MAXB, CHUNK):
        slots = range(first, first + CHUNK)
        keys = jnp.concatenate(
            [jnp.concatenate([key_at(0, m), key_at(1, m)], axis=1) for m in slots], axis=0
        )
        s = lax.dot_general(keys, w, (((1,), (1,)), ((), ())), preferred_element_type=jnp.float32)
        for m in slots:
            for n in range(2):
                part = s[(m - first) * BLK : (m - first + 1) * BLK, n * BLK : (n + 1) * BLK]
                if m == 0:
                    part = jnp.where(tri, part, -jnp.inf)
                s_ref[n, m * BLK : (m + 1) * BLK, :] = part
                top = over_rows(part, jnp.maximum)
                if m > 0:
                    top = top + bias(n, m)
                tops[n] = top if tops[n] is None else jnp.maximum(tops[n], top)
        yield


def weight_steps(tops, value_at, bias, s_ref, results):
    highest = [
        jnp.broadcast_to(jnp.max(t, axis=0, keepdims=True) * C, (8, BLK)) for t in tops
    ]
    total = [None, None]
    acc = [None, None]
    for first in range(0, MAXB, CHUNK):
        slots = range(first, first + CHUNK)
        for n in range(2):
            parts = []
            for m in slots:
                shift = highest[n] if m == 0 else highest[n] - bias(n, m)
                s = s_ref[n, m * BLK : (m + 1) * BLK, :].reshape(BLK // 8, 8, BLK)
                p = jnp.exp2(s * C - shift[None]).reshape(BLK, BLK)
                t = over_rows(p, jnp.add)
                total[n] = t if total[n] is None else total[n] + t
                parts.append(p.astype(jnp.bfloat16))
            values = jnp.concatenate([value_at(n, m) for m in slots], axis=1)
            o = jnp.dot(values, jnp.concatenate(parts, axis=0), preferred_element_type=jnp.float32)
            acc[n] = o if acc[n] is None else acc[n] + o
        yield
    for n in range(2):
        scale = 1.0 / jnp.sum(total[n], axis=0, keepdims=True)
        results.append((acc[n] * scale).T.astype(jnp.bfloat16))


def interleave(*steps):
    steps = list(steps)
    while steps:
        for one in list(steps):
            try:
                next(one)
            except StopIteration:
                steps.remove(one)


def kernel(
    ng, ny, q_ref, k_ref, v_ref, list_ref, count_ref, out_ref,
    buf_a, buf_b, own_kv, q_buf, o_buf, s_ref, k_buf, v_buf, lists, counts,
    kv_load, list_sem, q_own, o_own,
    plane_send, q_send, q_recv, o_send, o_recv,
    up_send, up_recv, side_send, side_recv,
):
    bufs = (buf_a, buf_b)
    c = lax.axis_index("core")
    chip = lax.axis_index("seq") * ny + lax.axis_index("y")
    g = chip // TEAM
    j = chip % TEAM
    last = ng - 1

    def at_chip(t):
        return {"seq": t // ny, "y": t % ny}

    def mate(k):
        return (j + k) % TEAM

    def block_of(group, member, core):
        return (group * TEAM + member) * 2 + core

    side = {"core": 1 - c}
    above = at_chip(jnp.minimum(chip + TEAM, ng * TEAM - 1))
    below = at_chip(jnp.maximum(chip - TEAM, 0))

    copies = [
        pltpu.make_async_copy(
            list_ref.at[pl.ds(pl.multiple_of(g * 8, 8), 8)], lists, list_sem.at[0]
        ),
        pltpu.make_async_copy(
            count_ref.at[pl.ds(pl.multiple_of(g * 8, 8), 8)], counts, list_sem.at[1]
        ),
    ]
    loads = [
        pltpu.make_async_copy(k_ref, k_buf, kv_load.at[0]),
        pltpu.make_async_copy(v_ref, v_buf, kv_load.at[1]),
    ]
    for copy in loads + copies:
        copy.start()

    barrier = pltpu.get_barrier_semaphore()
    for k in range(1, TEAM):
        pl.semaphore_signal(
            barrier, inc=1, device_id=at_chip(g * TEAM + mate(k)), device_id_type=MESH
        )
    pl.semaphore_signal(barrier, inc=1, device_id=side, device_id_type=MESH)

    @pl.when(g < last)
    def _():
        pl.semaphore_signal(barrier, inc=1, device_id=above, device_id_type=MESH)

    @pl.when(g > 0)
    def _():
        pl.semaphore_signal(barrier, inc=1, device_id=below, device_id_type=MESH)

    own_q = []
    for s in range(STAGES):
        copy = pltpu.make_async_copy(
            q_ref.at[:, pl.ds(pl.multiple_of((j * STAGES + s) * COLS, COLS), COLS)],
            q_buf.at[s, j], q_own.at[s],
        )
        copy.start()
        own_q.append(copy)
    for copy in loads:
        copy.wait()
    for h in range(KVH):
        own_kv[h, 0] = k_buf[:, h * D : (h + 1) * D]
        own_kv[h, 1] = v_buf[:, h * D : (h + 1) * D].T
    for s in range(STAGES):
        bufs[s][block_of(g, j, c)] = own_kv[j * STAGES + s]

    neighbours = 4 + (g < last).astype(jnp.int32) + (g > 0).astype(jnp.int32)
    pl.semaphore_wait(barrier, neighbours)

    def plane_copy(s, k):
        to = mate(k)
        return pltpu.make_async_remote_copy(
            src_ref=own_kv.at[to * STAGES + s],
            dst_ref=bufs[s].at[block_of(g, j, c)],
            send_sem=plane_send.at[s, k],
            recv_sem=up_recv.at[s, g, j],
            device_id=at_chip(g * TEAM + to),
            device_id_type=MESH,
        )

    def q_copy(s, k):
        to = mate(k)
        return pltpu.make_async_remote_copy(
            src_ref=q_ref.at[:, pl.ds(pl.multiple_of((to * STAGES + s) * COLS, COLS), COLS)],
            dst_ref=q_buf.at[s, j],
            send_sem=q_send.at[s, k],
            recv_sem=q_recv.at[s, j],
            device_id=at_chip(g * TEAM + to),
            device_id_type=MESH,
        )

    def q_arrival(s, k):
        frm = mate(k)
        return pltpu.make_async_remote_copy(
            src_ref=q_buf.at[s, frm],
            dst_ref=q_buf.at[s, frm],
            send_sem=q_send.at[s, k],
            recv_sem=q_recv.at[s, frm],
            device_id=at_chip(g * TEAM + frm),
            device_id_type=MESH,
        )

    def up_copy(s, group, member):
        piece = bufs[s].at[block_of(group, member, c)]
        return pltpu.make_async_remote_copy(
            src_ref=piece, dst_ref=piece,
            send_sem=up_send.at[s, group, member],
            recv_sem=up_recv.at[s, group, member],
            device_id=above,
            device_id_type=MESH,
        )

    def side_copy(s, core, group, member):
        piece = bufs[s].at[block_of(group, member, core)]
        return pltpu.make_async_remote_copy(
            src_ref=piece, dst_ref=piece,
            send_sem=side_send.at[s, group, member],
            recv_sem=side_recv.at[s, group, member],
            device_id=side,
            device_id_type=MESH,
        )

    def pass_on(s, group, member):
        pl.when(g < last)(up_copy(s, group, member).start)
        side_copy(s, c, group, member).start()

    def take(s, group, member):
        up_copy(s, group, member).wait_recv()
        pass_on(s, group, member)

    def take_group(s, group):
        def step(i, _):
            take(s, group, i)
            return 0

        lax.fori_loop(0, TEAM, step, 0)

    def take_below(s, low, high):
        def step(t, _):
            take(s, g - 1 - t // TEAM, t % TEAM)
            return 0

        lax.fori_loop(jnp.minimum(g, low) * TEAM, jnp.minimum(g, high) * TEAM, step, 0)

    def wait_sides(s):
        def step(t, _):
            side_copy(s, 1 - c, t // TEAM, t % TEAM).wait_recv()
            return 0

        lax.fori_loop(0, (g + 1) * TEAM, step, 0)

    for s in range(STAGES):
        for k in range(1, TEAM):
            plane_copy(s, k).start()
    pass_on(0, g, j)
    for k in range(1, TEAM):
        q_copy(0, k).start()
    for k in range(1, TEAM):
        take(0, g, mate(k))
    take_below(0, 0, ng)
    for k in range(1, TEAM):
        q_copy(1, k).start()
    pass_on(1, g, j)
    for k in range(1, TEAM):
        take(1, g, mate(k))
    wait_sides(0)
    for copy in copies:
        copy.wait()

    tri = lax.broadcasted_iota(jnp.int32, (BLK, BLK), 0) <= lax.broadcasted_iota(
        jnp.int32, (BLK, BLK), 1
    )

    def wait_queries(s):
        own_q[s].wait()
        for k in range(1, TEAM):
            q_arrival(s, k).wait_recv()

    def pair_of(s, t):
        member = mate(1 + t // PAIRS)
        pair = t % PAIRS
        row = 2 * member + c
        block = g * 8 + row
        slots = []
        limits = []
        for n in range(2):
            head = (j * STAGES + s) * GROUP + pair * 2 + n
            first = lists[row, 0, head]
            listed = [block]
            for m in range(1, MAXB):
                entry = lists[row, m, head]
                listed.append(jnp.where(entry == block, first, entry))
            slots.append([e.astype(jnp.uint32) for e in listed])
            limits.append(counts[row, head])

        def bias(n, m):
            return jnp.where(m < limits[n], 0.0, -jnp.inf).astype(jnp.float32)

        def piece(n, m, which):
            return bufs[s][slots[n][m], which]

        return member, pair, bias, piece

    def scores(s, t, side_ref, tops):
        member, pair, bias, piece = pair_of(s, t)
        queries = q_buf[s, member, :, pl.ds(pl.multiple_of(pair * 2 * D, 2 * D), 2 * D)]
        return score_steps(queries, lambda n, m: piece(n, m, 0), bias, tri, side_ref, tops)

    def weights(s, t, side_ref, tops, results):
        _, _, bias, piece = pair_of(s, t)
        return weight_steps(tops, lambda n, m: piece(n, m, 1), bias, side_ref, results)

    def out_local(s, part):
        mine = pl.multiple_of(part * 4 * D, 4 * D)
        cols = pl.multiple_of((j * STAGES + s) * COLS + part * 4 * D, 4 * D)
        return pltpu.make_async_copy(
            o_buf.at[s, j, :, pl.ds(mine, 4 * D)], out_ref.at[:, pl.ds(cols, 4 * D)],
            o_own.at[s, part],
        )

    def out_copy(s, member, part, owner):
        mine = pl.multiple_of(part * 4 * D, 4 * D)
        cols = pl.multiple_of((owner * STAGES + s) * COLS + part * 4 * D, 4 * D)
        return pltpu.make_async_remote_copy(
            src_ref=o_buf.at[s, member, :, pl.ds(mine, 4 * D)],
            dst_ref=out_ref.at[:, pl.ds(cols, 4 * D)],
            send_sem=o_send.at[s, member, part],
            recv_sem=o_recv.at[s, owner, part],
            device_id=at_chip(g * TEAM + member),
            device_id_type=MESH,
        )

    total = TEAM * PAIRS
    rounds = total // 2

    def attend(s, after):
        tops = [None, None]
        interleave(scores(s, 0, s_ref.at[0], tops))

        def two_pairs(i, tops, more):
            for half in range(2):
                t = 2 * i + half
                later = [None, None]
                results = []
                steps = [weights(s, t, s_ref.at[half], list(tops), results)]
                if more or half == 0:
                    steps.insert(0, scores(s, t + 1, s_ref.at[1 - half], later))
                interleave(*steps)
                member = mate(1 + t // PAIRS)
                cols = pl.ds(pl.multiple_of(t % PAIRS * 2 * D, 2 * D), 2 * D)
                o_buf[s, member, :, cols] = jnp.concatenate(results, axis=1)
                tops = tuple(later)
            return tops

        def step(i, tops):
            tops = two_pairs(i, tops, True)
            member = mate(1 + i // PARTS)
            part = i % PARTS
            pl.when(member != j)(out_copy(s, member, part, j).start)
            pl.when(member == j)(out_local(s, part).start)
            after(i)
            return tops

        tops = lax.fori_loop(0, rounds - 1, step, tuple(tops))
        two_pairs(rounds - 1, tops, False)
        out_local(s, PARTS - 1).start()

    def passed(i):
        return jnp.where(g < last, jnp.where(i < 4, (i + 1) // 2, ng), jnp.maximum(i, 0) // 3)

    wait_queries(0)
    attend(0, lambda i: take_below(1, passed(i - 1), passed(i)))
    take_below(1, passed(rounds - 2), ng)
    wait_sides(1)
    wait_queries(1)
    attend(1, lambda i: None)

    for s in range(STAGES):
        for k in range(1, TEAM):
            plane_copy(s, k).wait_send()
            q_copy(s, k).wait_send()
            for part in range(PARTS):
                out_copy(s, mate(k), part, j).wait_send()
                out_copy(s, j, part, mate(k)).wait_recv()
        for part in range(PARTS):
            out_local(s, part).wait()

        def step(t, _):
            pl.when(g < last)(up_copy(s, t // TEAM, t % TEAM).wait_send)
            side_copy(s, c, t // TEAM, t % TEAM).wait_send()
            return 0

        lax.fori_loop(0, (g + 1) * TEAM, step, 0)


def fused(ng, ny, q, k, v, block_list, block_count):
    anywhere = pl.BlockSpec(memory_space=pl.ANY)
    buf = pltpu.VMEM((ng * 2 * TEAM, 2, BLK, D), jnp.bfloat16)
    dma = pltpu.SemaphoreType.DMA
    return pl.pallas_call(
        functools.partial(kernel, ng, ny),
        in_specs=[anywhere] * 5,
        out_specs=anywhere,
        out_shape=jax.ShapeDtypeStruct(q.shape, jnp.bfloat16),
        scratch_shapes=[
            buf,
            buf,
            pltpu.VMEM((KVH, 2, BLK, D), jnp.bfloat16),
            pltpu.VMEM((STAGES, TEAM, BLK, COLS), jnp.bfloat16),
            pltpu.VMEM((STAGES, TEAM, BLK, COLS), jnp.bfloat16),
            pltpu.VMEM((2, 2, MAXB * BLK, BLK), jnp.float32),
            pltpu.VMEM((BLK, KVH * D), jnp.bfloat16),
            pltpu.VMEM((BLK, KVH * D), jnp.bfloat16),
            pltpu.SMEM((2 * TEAM, MAXB, H), jnp.int32),
            pltpu.SMEM((2 * TEAM, H), jnp.int32),
            dma((2,)),
            dma((2,)),
            dma((STAGES,)),
            dma((STAGES, PARTS)),
            dma((STAGES, TEAM)),
            dma((STAGES, TEAM)),
            dma((STAGES, TEAM)),
            dma((STAGES, TEAM, PARTS)),
            dma((STAGES, TEAM, PARTS)),
            dma((STAGES, ng, TEAM)),
            dma((STAGES, ng, TEAM)),
            dma((STAGES, ng, TEAM)),
            dma((STAGES, ng, TEAM)),
        ],
        compiler_params=pltpu.CompilerParams(
            collective_id=0, has_side_effects=True, vmem_limit_bytes=48 * 1024 * 1024
        ),
        name="heads_attend",
    )(*(pltpu.with_memory_space_constraint(x, pltpu.HBM) for x in (q, k, v, block_list, block_count)))


def shards(q, k, v, block_list, block_count):
    ny = lax.axis_size("y")
    ng = lax.axis_size("seq") * ny // TEAM
    return fused(ng, ny, q, k, v, block_list.transpose(1, 2, 0), block_count.T)


def solution(mesh):
    n_seq, n_qblk = mesh.devices.shape
    fine = Mesh(mesh.devices.reshape(n_seq, n_qblk // 2, 2), ("seq", "y", "core"))
    rows = P(("seq", "y", "core"), None)
    return jax.shard_map(
        shards,
        mesh=fine,
        in_specs=(rows, rows, rows, P(), P()),
        out_specs=rows,
        check_vma=False,
    )
```

```python
import functools

import jax
import jax.numpy as jnp
from jax import lax
from jax.experimental import pallas as pl
from jax.experimental.pallas import tpu as pltpu
from jax.sharding import Mesh, PartitionSpec as P

H = 64
KVH = 8
D = 128
BLK = 128
MAXB = 16
GROUP = H // KVH
TEAM = 4
STAGES = KVH // TEAM
PAIRS = GROUP // 2
PARTS = PAIRS // 2
COLS = GROUP * D
LOG2E = 1.4426950408889634
C = D ** (-0.5) * LOG2E
CHUNK = 2
MESH = pl.DeviceIdType.MESH


def over_rows(x, op):
    n = x.shape[0] // 8
    x = x.reshape(n, 8, x.shape[1])
    while n > 1:
        n //= 2
        x = op(x[:n], x[n:])
    return x[0]


def score_steps(queries, key_at, bias, tri, s_ref, tops):
    zero = jnp.zeros((BLK, D), jnp.bfloat16)
    w = jnp.concatenate(
        [
            jnp.concatenate([queries[:, :D], zero], axis=1),
            jnp.concatenate([zero, queries[:, D:]], axis=1),
        ],
        axis=0,
    )
    for first in range(0, MAXB, CHUNK):
        slots = range(first, first + CHUNK)
        keys = jnp.concatenate(
            [jnp.concatenate([key_at(0, m), key_at(1, m)], axis=1) for m in slots], axis=0
        )
        s = lax.dot_general(keys, w, (((1,), (1,)), ((), ())), preferred_element_type=jnp.float32)
        for m in slots:
            for n in range(2):
                part = s[(m - first) * BLK : (m - first + 1) * BLK, n * BLK : (n + 1) * BLK]
                if m == 0:
                    part = jnp.where(tri, part, -jnp.inf)
                s_ref[n, m * BLK : (m + 1) * BLK, :] = part
                top = over_rows(part, jnp.maximum)
                if m > 0:
                    top = top + bias(n, m)
                tops[n] = top if tops[n] is None else jnp.maximum(tops[n], top)
        yield


def weight_steps(tops, value_at, bias, s_ref, results):
    highest = [
        jnp.broadcast_to(jnp.max(t, axis=0, keepdims=True) * C, (8, BLK)) for t in tops
    ]
    total = [None, None]
    acc = [None, None]
    for first in range(0, MAXB, CHUNK):
        slots = range(first, first + CHUNK)
        for n in range(2):
            parts = []
            for m in slots:
                shift = highest[n] if m == 0 else highest[n] - bias(n, m)
                s = s_ref[n, m * BLK : (m + 1) * BLK, :].reshape(BLK // 8, 8, BLK)
                p = jnp.exp2(s * C - shift[None]).reshape(BLK, BLK)
                t = over_rows(p, jnp.add)
                total[n] = t if total[n] is None else total[n] + t
                parts.append(p.astype(jnp.bfloat16))
            values = jnp.concatenate([value_at(n, m) for m in slots], axis=1)
            o = jnp.dot(values, jnp.concatenate(parts, axis=0), preferred_element_type=jnp.float32)
            acc[n] = o if acc[n] is None else acc[n] + o
        yield
    for n in range(2):
        scale = 1.0 / jnp.sum(total[n], axis=0, keepdims=True)
        results.append((acc[n] * scale).T.astype(jnp.bfloat16))


def interleave(*steps):
    steps = list(steps)
    while steps:
        for one in list(steps):
            try:
                next(one)
            except StopIteration:
                steps.remove(one)


def kernel(
    ng, ny, q_ref, k_ref, v_ref, list_ref, count_ref, out_ref,
    buf_a, buf_b, own_kv, q_buf, o_buf, s_ref, k_buf, v_buf, lists, counts,
    kv_load, list_sem, q_own, o_own,
    plane_send, q_send, q_recv, o_send, o_recv,
    up_send, up_recv, side_send, side_recv,
):
    bufs = (buf_a, buf_b)
    c = lax.axis_index("core")
    chip = lax.axis_index("seq") * ny + lax.axis_index("y")
    g = chip // TEAM
    j = chip % TEAM
    last = ng - 1

    def at_chip(t):
        return {"seq": t // ny, "y": t % ny}

    def mate(k):
        k = k % TEAM
        side_b = 2 * (j // 2) + 1 - j % 2
        return jnp.where(
            k == 0, j, jnp.where(k == 1, 3 - j, jnp.where(k == 2, (j + 2) % TEAM, side_b))
        )

    def block_of(group, member, core):
        return (group * TEAM + member) * 2 + core

    side = {"core": 1 - c}
    above = at_chip(jnp.minimum(chip + TEAM, ng * TEAM - 1))
    below = at_chip(jnp.maximum(chip - TEAM, 0))

    copies = [
        pltpu.make_async_copy(
            list_ref.at[pl.ds(pl.multiple_of(g * 8, 8), 8)], lists, list_sem.at[0]
        ),
        pltpu.make_async_copy(
            count_ref.at[pl.ds(pl.multiple_of(g * 8, 8), 8)], counts, list_sem.at[1]
        ),
    ]
    loads = [
        pltpu.make_async_copy(k_ref, k_buf, kv_load.at[0]),
        pltpu.make_async_copy(v_ref, v_buf, kv_load.at[1]),
    ]
    for copy in loads + copies:
        copy.start()

    barrier = pltpu.get_barrier_semaphore()
    for k in range(1, TEAM):
        pl.semaphore_signal(
            barrier, inc=1, device_id=at_chip(g * TEAM + mate(k)), device_id_type=MESH
        )
    pl.semaphore_signal(barrier, inc=1, device_id=side, device_id_type=MESH)

    @pl.when(g < last)
    def _():
        pl.semaphore_signal(barrier, inc=1, device_id=above, device_id_type=MESH)

    @pl.when(g > 0)
    def _():
        pl.semaphore_signal(barrier, inc=1, device_id=below, device_id_type=MESH)

    own_q = []
    for s in range(STAGES):
        copy = pltpu.make_async_copy(
            q_ref.at[:, pl.ds(pl.multiple_of((j * STAGES + s) * COLS, COLS), COLS)],
            q_buf.at[s, j], q_own.at[s],
        )
        copy.start()
        own_q.append(copy)
    for copy in loads:
        copy.wait()
    for h in range(KVH):
        own_kv[h, 0] = k_buf[:, h * D : (h + 1) * D]
        own_kv[h, 1] = v_buf[:, h * D : (h + 1) * D].T
    for s in range(STAGES):
        bufs[s][block_of(g, j, c)] = own_kv[j * STAGES + s]

    neighbours = 4 + (g < last).astype(jnp.int32) + (g > 0).astype(jnp.int32)
    pl.semaphore_wait(barrier, neighbours)

    def plane_copy(s, k):
        to = mate(k)
        return pltpu.make_async_remote_copy(
            src_ref=own_kv.at[to * STAGES + s],
            dst_ref=bufs[s].at[block_of(g, j, c)],
            send_sem=plane_send.at[s, k],
            recv_sem=up_recv.at[s, g, j],
            device_id=at_chip(g * TEAM + to),
            device_id_type=MESH,
        )

    def q_copy(s, k):
        to = mate(k)
        return pltpu.make_async_remote_copy(
            src_ref=q_ref.at[:, pl.ds(pl.multiple_of((to * STAGES + s) * COLS, COLS), COLS)],
            dst_ref=q_buf.at[s, j],
            send_sem=q_send.at[s, k],
            recv_sem=q_recv.at[s, j],
            device_id=at_chip(g * TEAM + to),
            device_id_type=MESH,
        )

    def q_arrival(s, k):
        frm = mate(k)
        return pltpu.make_async_remote_copy(
            src_ref=q_buf.at[s, frm],
            dst_ref=q_buf.at[s, frm],
            send_sem=q_send.at[s, k],
            recv_sem=q_recv.at[s, frm],
            device_id=at_chip(g * TEAM + frm),
            device_id_type=MESH,
        )

    def up_copy(s, group, member):
        piece = bufs[s].at[block_of(group, member, c)]
        return pltpu.make_async_remote_copy(
            src_ref=piece, dst_ref=piece,
            send_sem=up_send.at[s, group, member],
            recv_sem=up_recv.at[s, group, member],
            device_id=above,
            device_id_type=MESH,
        )

    def side_copy(s, core, group, member):
        piece = bufs[s].at[block_of(group, member, core)]
        return pltpu.make_async_remote_copy(
            src_ref=piece, dst_ref=piece,
            send_sem=side_send.at[s, group, member],
            recv_sem=side_recv.at[s, group, member],
            device_id=side,
            device_id_type=MESH,
        )

    def pass_on(s, group, member):
        pl.when(g < last)(up_copy(s, group, member).start)
        side_copy(s, c, group, member).start()

    def take(s, group, member):
        up_copy(s, group, member).wait_recv()
        pass_on(s, group, member)

    def take_group(s, group):
        def step(i, _):
            take(s, group, i)
            return 0

        lax.fori_loop(0, TEAM, step, 0)

    def take_below(s, low, high):
        def step(t, _):
            take(s, g - 1 - t // TEAM, t % TEAM)
            return 0

        lax.fori_loop(jnp.minimum(g, low) * TEAM, jnp.minimum(g, high) * TEAM, step, 0)

    def wait_sides(s):
        def step(t, _):
            side_copy(s, 1 - c, t // TEAM, t % TEAM).wait_recv()
            return 0

        lax.fori_loop(0, (g + 1) * TEAM, step, 0)

    pass_on(0, g, j)
    for s in range(STAGES):
        for k in range(1, TEAM):
            plane_copy(s, k).start()
    pass_on(1, g, j)
    for k in range(1, TEAM):
        q_copy(0, k).start()
    for k in range(1, TEAM):
        take(0, g, mate(k))
    take_below(0, 0, ng)
    for k in range(1, TEAM):
        q_copy(1, k).start()
    for k in range(1, TEAM):
        take(1, g, mate(k))
    wait_sides(0)
    for copy in copies:
        copy.wait()

    tri = lax.broadcasted_iota(jnp.int32, (BLK, BLK), 0) <= lax.broadcasted_iota(
        jnp.int32, (BLK, BLK), 1
    )

    def wait_queries(s):
        own_q[s].wait()
        for k in range(1, TEAM):
            q_arrival(s, k).wait_recv()

    def pair_of(s, t):
        member = mate(1 + t // PAIRS)
        pair = t % PAIRS
        row = 2 * member + c
        block = g * 8 + row
        slots = []
        limits = []
        for n in range(2):
            head = (j * STAGES + s) * GROUP + pair * 2 + n
            first = lists[row, 0, head]
            listed = [block]
            for m in range(1, MAXB):
                entry = lists[row, m, head]
                listed.append(jnp.where(entry == block, first, entry))
            slots.append([e.astype(jnp.uint32) for e in listed])
            limits.append(counts[row, head])

        def bias(n, m):
            return jnp.where(m < limits[n], 0.0, -jnp.inf).astype(jnp.float32)

        def piece(n, m, which):
            return bufs[s][slots[n][m], which]

        return member, pair, bias, piece

    def scores(s, t, side_ref, tops):
        member, pair, bias, piece = pair_of(s, t)
        queries = q_buf[s, member, :, pl.ds(pl.multiple_of(pair * 2 * D, 2 * D), 2 * D)]
        return score_steps(queries, lambda n, m: piece(n, m, 0), bias, tri, side_ref, tops)

    def weights(s, t, side_ref, tops, results):
        _, _, bias, piece = pair_of(s, t)
        return weight_steps(tops, lambda n, m: piece(n, m, 1), bias, side_ref, results)

    def out_local(s, part):
        mine = pl.multiple_of(part * 4 * D, 4 * D)
        cols = pl.multiple_of((j * STAGES + s) * COLS + part * 4 * D, 4 * D)
        return pltpu.make_async_copy(
            o_buf.at[s, j, :, pl.ds(mine, 4 * D)], out_ref.at[:, pl.ds(cols, 4 * D)],
            o_own.at[s, part],
        )

    def out_copy(s, member, part, owner):
        mine = pl.multiple_of(part * 4 * D, 4 * D)
        cols = pl.multiple_of((owner * STAGES + s) * COLS + part * 4 * D, 4 * D)
        return pltpu.make_async_remote_copy(
            src_ref=o_buf.at[s, member, :, pl.ds(mine, 4 * D)],
            dst_ref=out_ref.at[:, pl.ds(cols, 4 * D)],
            send_sem=o_send.at[s, member, part],
            recv_sem=o_recv.at[s, owner, part],
            device_id=at_chip(g * TEAM + member),
            device_id_type=MESH,
        )

    total = TEAM * PAIRS
    rounds = total // 2

    def attend(s, after):
        tops = [None, None]
        interleave(scores(s, 0, s_ref.at[0], tops))

        def two_pairs(i, tops, more):
            for half in range(2):
                t = 2 * i + half
                later = [None, None]
                results = []
                steps = [weights(s, t, s_ref.at[half], list(tops), results)]
                if more or half == 0:
                    steps.insert(0, scores(s, t + 1, s_ref.at[1 - half], later))
                interleave(*steps)
                member = mate(1 + t // PAIRS)
                cols = pl.ds(pl.multiple_of(t % PAIRS * 2 * D, 2 * D), 2 * D)
                o_buf[s, member, :, cols] = jnp.concatenate(results, axis=1)
                tops = tuple(later)
            return tops

        def step(i, tops):
            tops = two_pairs(i, tops, True)
            member = mate(1 + i // PARTS)
            part = i % PARTS
            pl.when(member != j)(out_copy(s, member, part, j).start)
            pl.when(member == j)(out_local(s, part).start)
            after(i)
            return tops

        tops = lax.fori_loop(0, rounds - 1, step, tuple(tops))
        two_pairs(rounds - 1, tops, False)
        out_local(s, PARTS - 1).start()

    def passed(i):
        return jnp.where(g < last, jnp.where(i < 4, (i + 1) // 2, ng), jnp.maximum(i, 0) // 3)

    wait_queries(0)
    attend(0, lambda i: take_below(1, passed(i - 1), passed(i)))
    take_below(1, passed(rounds - 2), ng)
    wait_sides(1)
    wait_queries(1)
    attend(1, lambda i: None)

    for s in range(STAGES):
        for k in range(1, TEAM):
            plane_copy(s, k).wait_send()
            q_copy(s, k).wait_send()
            for part in range(PARTS):
                out_copy(s, mate(k), part, j).wait_send()
                out_copy(s, j, part, mate(k)).wait_recv()
        for part in range(PARTS):
            out_local(s, part).wait()

        def step(t, _):
            pl.when(g < last)(up_copy(s, t // TEAM, t % TEAM).wait_send)
            side_copy(s, c, t // TEAM, t % TEAM).wait_send()
            return 0

        lax.fori_loop(0, (g + 1) * TEAM, step, 0)


def fused(ng, ny, q, k, v, block_list, block_count):
    anywhere = pl.BlockSpec(memory_space=pl.ANY)
    buf = pltpu.VMEM((ng * 2 * TEAM, 2, BLK, D), jnp.bfloat16)
    dma = pltpu.SemaphoreType.DMA
    return pl.pallas_call(
        functools.partial(kernel, ng, ny),
        in_specs=[anywhere] * 5,
        out_specs=anywhere,
        out_shape=jax.ShapeDtypeStruct(q.shape, jnp.bfloat16),
        scratch_shapes=[
            buf,
            buf,
            pltpu.VMEM((KVH, 2, BLK, D), jnp.bfloat16),
            pltpu.VMEM((STAGES, TEAM, BLK, COLS), jnp.bfloat16),
            pltpu.VMEM((STAGES, TEAM, BLK, COLS), jnp.bfloat16),
            pltpu.VMEM((2, 2, MAXB * BLK, BLK), jnp.float32),
            pltpu.VMEM((BLK, KVH * D), jnp.bfloat16),
            pltpu.VMEM((BLK, KVH * D), jnp.bfloat16),
            pltpu.SMEM((2 * TEAM, MAXB, H), jnp.int32),
            pltpu.SMEM((2 * TEAM, H), jnp.int32),
            dma((2,)),
            dma((2,)),
            dma((STAGES,)),
            dma((STAGES, PARTS)),
            dma((STAGES, TEAM)),
            dma((STAGES, TEAM)),
            dma((STAGES, TEAM)),
            dma((STAGES, TEAM, PARTS)),
            dma((STAGES, TEAM, PARTS)),
            dma((STAGES, ng, TEAM)),
            dma((STAGES, ng, TEAM)),
            dma((STAGES, ng, TEAM)),
            dma((STAGES, ng, TEAM)),
        ],
        compiler_params=pltpu.CompilerParams(
            collective_id=0, has_side_effects=True, vmem_limit_bytes=48 * 1024 * 1024
        ),
        name="heads_attend",
    )(*(pltpu.with_memory_space_constraint(x, pltpu.HBM) for x in (q, k, v, block_list, block_count)))


def shards(q, k, v, block_list, block_count):
    ny = lax.axis_size("y")
    ng = lax.axis_size("seq") * ny // TEAM
    return fused(ng, ny, q, k, v, block_list.transpose(1, 2, 0), block_count.T)


def solution(mesh):
    n_seq, n_qblk = mesh.devices.shape
    fine = Mesh(mesh.devices.reshape(n_seq, n_qblk // 2, 2), ("seq", "y", "core"))
    rows = P(("seq", "y", "core"), None)
    return jax.shard_map(
        shards,
        mesh=fine,
        in_specs=(rows, rows, rows, P(), P()),
        out_specs=rows,
        check_vma=False,
    )
```

```python
import functools

import jax
import jax.numpy as jnp
from jax import lax
from jax.experimental import pallas as pl
from jax.experimental.pallas import tpu as pltpu
from jax.sharding import Mesh, PartitionSpec as P

H = 64
KVH = 8
D = 128
BLK = 128
MAXB = 16
GROUP = H // KVH
TEAM = 4
STAGES = KVH // TEAM
PAIRS = GROUP // 2
PARTS = PAIRS // 2
COLS = GROUP * D
LOG2E = 1.4426950408889634
C = D ** (-0.5) * LOG2E
CHUNK = 2
MESH = pl.DeviceIdType.MESH


def over_rows(x, op):
    n = x.shape[0] // 8
    x = x.reshape(n, 8, x.shape[1])
    while n > 1:
        n //= 2
        x = op(x[:n], x[n:])
    return x[0]


def score_steps(queries, key_at, bias, tri, s_ref, tops):
    zero = jnp.zeros((BLK, D), jnp.bfloat16)
    w = jnp.concatenate(
        [
            jnp.concatenate([queries[:, :D], zero], axis=1),
            jnp.concatenate([zero, queries[:, D:]], axis=1),
        ],
        axis=0,
    )
    for first in range(0, MAXB, CHUNK):
        slots = range(first, first + CHUNK)
        keys = jnp.concatenate(
            [jnp.concatenate([key_at(0, m), key_at(1, m)], axis=1) for m in slots], axis=0
        )
        s = lax.dot_general(keys, w, (((1,), (1,)), ((), ())), preferred_element_type=jnp.float32)
        for m in slots:
            for n in range(2):
                part = s[(m - first) * BLK : (m - first + 1) * BLK, n * BLK : (n + 1) * BLK]
                if m == 0:
                    part = jnp.where(tri, part, -jnp.inf)
                s_ref[n, m * BLK : (m + 1) * BLK, :] = part
                top = over_rows(part, jnp.maximum)
                if m > 0:
                    top = top + bias(n, m)
                tops[n] = top if tops[n] is None else jnp.maximum(tops[n], top)
        yield


def weight_steps(tops, value_at, bias, s_ref, results):
    highest = [
        jnp.broadcast_to(jnp.max(t, axis=0, keepdims=True) * C, (8, BLK)) for t in tops
    ]
    total = [None, None]
    acc = [None, None]
    for first in range(0, MAXB, CHUNK):
        slots = range(first, first + CHUNK)
        for n in range(2):
            parts = []
            for m in slots:
                shift = highest[n] if m == 0 else highest[n] - bias(n, m)
                s = s_ref[n, m * BLK : (m + 1) * BLK, :].reshape(BLK // 8, 8, BLK)
                p = jnp.exp2(s * C - shift[None]).reshape(BLK, BLK)
                t = over_rows(p, jnp.add)
                total[n] = t if total[n] is None else total[n] + t
                parts.append(p.astype(jnp.bfloat16))
            values = jnp.concatenate([value_at(n, m) for m in slots], axis=1)
            o = jnp.dot(values, jnp.concatenate(parts, axis=0), preferred_element_type=jnp.float32)
            acc[n] = o if acc[n] is None else acc[n] + o
        yield
    for n in range(2):
        scale = 1.0 / jnp.sum(total[n], axis=0, keepdims=True)
        results.append((acc[n] * scale).T.astype(jnp.bfloat16))


def interleave(*steps):
    steps = list(steps)
    while steps:
        for one in list(steps):
            try:
                next(one)
            except StopIteration:
                steps.remove(one)


def kernel(
    ng, ny, q_ref, k_ref, v_ref, list_ref, count_ref, out_ref,
    buf_a, buf_b, own_kv, q_buf, o_buf, s_ref, k_buf, v_buf, lists, counts,
    kv_load, list_sem, q_own, o_own,
    plane_send, q_send, q_recv, o_send, o_recv,
    up_send, up_recv, side_send, side_recv,
):
    bufs = (buf_a, buf_b)
    c = lax.axis_index("core")
    chip = lax.axis_index("seq") * ny + lax.axis_index("y")
    g = chip // TEAM
    j = chip % TEAM
    last = ng - 1

    def at_chip(t):
        return {"seq": t // ny, "y": t % ny}

    def mate(k):
        k = k % TEAM
        side_b = 2 * (j // 2) + 1 - j % 2
        return jnp.where(
            k == 0, j, jnp.where(k == 1, 3 - j, jnp.where(k == 2, (j + 2) % TEAM, side_b))
        )

    def block_of(group, member, core):
        return (group * TEAM + member) * 2 + core

    side = {"core": 1 - c}
    above = at_chip(jnp.minimum(chip + TEAM, ng * TEAM - 1))
    below = at_chip(jnp.maximum(chip - TEAM, 0))

    copies = [
        pltpu.make_async_copy(
            list_ref.at[pl.ds(pl.multiple_of(g * 8, 8), 8)], lists, list_sem.at[0]
        ),
        pltpu.make_async_copy(
            count_ref.at[pl.ds(pl.multiple_of(g * 8, 8), 8)], counts, list_sem.at[1]
        ),
    ]
    loads = [
        pltpu.make_async_copy(k_ref, k_buf, kv_load.at[0]),
        pltpu.make_async_copy(v_ref, v_buf, kv_load.at[1]),
    ]
    for copy in loads + copies:
        copy.start()

    barrier = pltpu.get_barrier_semaphore()
    for k in range(1, TEAM):
        pl.semaphore_signal(
            barrier, inc=1, device_id=at_chip(g * TEAM + mate(k)), device_id_type=MESH
        )
    pl.semaphore_signal(barrier, inc=1, device_id=side, device_id_type=MESH)

    @pl.when(g < last)
    def _():
        pl.semaphore_signal(barrier, inc=1, device_id=above, device_id_type=MESH)

    @pl.when(g > 0)
    def _():
        pl.semaphore_signal(barrier, inc=1, device_id=below, device_id_type=MESH)

    own_q = []
    for s in range(STAGES):
        copy = pltpu.make_async_copy(
            q_ref.at[:, pl.ds(pl.multiple_of((j * STAGES + s) * COLS, COLS), COLS)],
            q_buf.at[s, j], q_own.at[s],
        )
        copy.start()
        own_q.append(copy)
    for copy in loads:
        copy.wait()
    for h in range(KVH):
        own_kv[h, 0] = k_buf[:, h * D : (h + 1) * D]
        own_kv[h, 1] = v_buf[:, h * D : (h + 1) * D].T
    for s in range(STAGES):
        bufs[s][block_of(g, j, c)] = own_kv[j * STAGES + s]

    neighbours = 4 + (g < last).astype(jnp.int32) + (g > 0).astype(jnp.int32)
    pl.semaphore_wait(barrier, neighbours)

    def plane_copy(s, k):
        to = mate(k)
        return pltpu.make_async_remote_copy(
            src_ref=own_kv.at[to * STAGES + s],
            dst_ref=bufs[s].at[block_of(g, j, c)],
            send_sem=plane_send.at[s, k],
            recv_sem=up_recv.at[s, g, j],
            device_id=at_chip(g * TEAM + to),
            device_id_type=MESH,
        )

    def q_copy(s, k):
        to = mate(k)
        return pltpu.make_async_remote_copy(
            src_ref=q_ref.at[:, pl.ds(pl.multiple_of((to * STAGES + s) * COLS, COLS), COLS)],
            dst_ref=q_buf.at[s, j],
            send_sem=q_send.at[s, k],
            recv_sem=q_recv.at[s, j],
            device_id=at_chip(g * TEAM + to),
            device_id_type=MESH,
        )

    def q_arrival(s, k):
        frm = mate(k)
        return pltpu.make_async_remote_copy(
            src_ref=q_buf.at[s, frm],
            dst_ref=q_buf.at[s, frm],
            send_sem=q_send.at[s, k],
            recv_sem=q_recv.at[s, frm],
            device_id=at_chip(g * TEAM + frm),
            device_id_type=MESH,
        )

    def up_copy(s, group, member):
        piece = bufs[s].at[block_of(group, member, c)]
        return pltpu.make_async_remote_copy(
            src_ref=piece, dst_ref=piece,
            send_sem=up_send.at[s, group, member],
            recv_sem=up_recv.at[s, group, member],
            device_id=above,
            device_id_type=MESH,
        )

    def side_copy(s, core, group, member):
        piece = bufs[s].at[block_of(group, member, core)]
        return pltpu.make_async_remote_copy(
            src_ref=piece, dst_ref=piece,
            send_sem=side_send.at[s, group, member],
            recv_sem=side_recv.at[s, group, member],
            device_id=side,
            device_id_type=MESH,
        )

    def pass_on(s, group, member):
        pl.when(g < last)(up_copy(s, group, member).start)
        side_copy(s, c, group, member).start()

    def take(s, group, member):
        up_copy(s, group, member).wait_recv()
        pass_on(s, group, member)

    def take_group(s, group):
        def step(i, _):
            take(s, group, i)
            return 0

        lax.fori_loop(0, TEAM, step, 0)

    def take_below(s, low, high):
        def step(t, _):
            take(s, g - 1 - t // TEAM, t % TEAM)
            return 0

        lax.fori_loop(jnp.minimum(g, low) * TEAM, jnp.minimum(g, high) * TEAM, step, 0)

    def wait_sides(s):
        def step(t, _):
            side_copy(s, 1 - c, t // TEAM, t % TEAM).wait_recv()
            return 0

        lax.fori_loop(0, (g + 1) * TEAM, step, 0)

    pass_on(0, g, j)
    for s in range(STAGES):
        for k in range(1, TEAM):
            plane_copy(s, k).start()
    pass_on(1, g, j)
    for k in range(1, TEAM):
        q_copy(0, k).start()
    for k in range(1, TEAM):
        take(0, g, mate(k))
    take_below(0, 0, ng)
    for k in range(1, TEAM):
        q_copy(1, k).start()
    for k in range(1, TEAM):
        take(1, g, mate(k))
    wait_sides(0)
    for copy in copies:
        copy.wait()

    tri = lax.broadcasted_iota(jnp.int32, (BLK, BLK), 0) <= lax.broadcasted_iota(
        jnp.int32, (BLK, BLK), 1
    )

    def wait_queries(s):
        own_q[s].wait()
        for k in range(1, TEAM):
            q_arrival(s, k).wait_recv()

    def pair_of(s, t):
        member = mate(1 + t // PAIRS)
        pair = t % PAIRS
        row = 2 * member + c
        block = g * 8 + row
        slots = []
        limits = []
        for n in range(2):
            head = (j * STAGES + s) * GROUP + pair * 2 + n
            first = lists[row, 0, head]
            listed = [block]
            for m in range(1, MAXB):
                entry = lists[row, m, head]
                listed.append(jnp.where(entry == block, first, entry))
            slots.append([e.astype(jnp.uint32) for e in listed])
            limits.append(counts[row, head])

        def bias(n, m):
            return jnp.where(m < limits[n], 0.0, -jnp.inf).astype(jnp.float32)

        def piece(n, m, which):
            return bufs[s][slots[n][m], which]

        return member, pair, bias, piece

    def scores(s, t, side_ref, tops):
        member, pair, bias, piece = pair_of(s, t)
        queries = q_buf[s, member, :, pl.ds(pl.multiple_of(pair * 2 * D, 2 * D), 2 * D)]
        return score_steps(queries, lambda n, m: piece(n, m, 0), bias, tri, side_ref, tops)

    def weights(s, t, side_ref, tops, results):
        _, _, bias, piece = pair_of(s, t)
        return weight_steps(tops, lambda n, m: piece(n, m, 1), bias, side_ref, results)

    def out_local(s, part):
        mine = pl.multiple_of(part * 4 * D, 4 * D)
        cols = pl.multiple_of((j * STAGES + s) * COLS + part * 4 * D, 4 * D)
        return pltpu.make_async_copy(
            o_buf.at[s, j, :, pl.ds(mine, 4 * D)], out_ref.at[:, pl.ds(cols, 4 * D)],
            o_own.at[s, part],
        )

    def out_copy(s, member, part, owner):
        mine = pl.multiple_of(part * 4 * D, 4 * D)
        cols = pl.multiple_of((owner * STAGES + s) * COLS + part * 4 * D, 4 * D)
        return pltpu.make_async_remote_copy(
            src_ref=o_buf.at[s, member, :, pl.ds(mine, 4 * D)],
            dst_ref=out_ref.at[:, pl.ds(cols, 4 * D)],
            send_sem=o_send.at[s, member, part],
            recv_sem=o_recv.at[s, owner, part],
            device_id=at_chip(g * TEAM + member),
            device_id_type=MESH,
        )

    total = TEAM * PAIRS
    rounds = total // 2

    def attend(s, after):
        tops = [None, None]
        interleave(scores(s, 0, s_ref.at[0], tops))

        def two_pairs(i, tops, more):
            for half in range(2):
                t = 2 * i + half
                later = [None, None]
                results = []
                steps = [weights(s, t, s_ref.at[half], list(tops), results)]
                if more or half == 0:
                    steps.insert(0, scores(s, t + 1, s_ref.at[1 - half], later))
                interleave(*steps)
                member = mate(1 + t // PAIRS)
                cols = pl.ds(pl.multiple_of(t % PAIRS * 2 * D, 2 * D), 2 * D)
                o_buf[s, member, :, cols] = jnp.concatenate(results, axis=1)
                tops = tuple(later)
            return tops

        def step(i, tops):
            tops = two_pairs(i, tops, True)
            member = mate(1 + i // PARTS)
            part = i % PARTS
            pl.when(member != j)(out_copy(s, member, part, j).start)
            pl.when(member == j)(out_local(s, part).start)
            after(i)
            return tops

        tops = lax.fori_loop(0, rounds - 1, step, tuple(tops))
        two_pairs(rounds - 1, tops, False)
        out_local(s, PARTS - 1).start()

    def passed(i):
        return jnp.where(g < last, jnp.where(i < 4, (i + 1) // 2, ng), jnp.maximum(i, 0) // 3)

    wait_queries(0)
    attend(0, lambda i: take_below(1, passed(i - 1), passed(i)))
    take_below(1, passed(rounds - 2), ng)
    wait_sides(1)
    wait_queries(1)
    attend(1, lambda i: None)

    for s in range(STAGES):
        for k in range(1, TEAM):
            plane_copy(s, k).wait_send()
            q_copy(s, k).wait_send()

        def step(t, _):
            pl.when(g < last)(up_copy(s, t // TEAM, t % TEAM).wait_send)
            side_copy(s, c, t // TEAM, t % TEAM).wait_send()
            return 0

        lax.fori_loop(0, (g + 1) * TEAM, step, 0)
    for s in range(STAGES):
        for part in range(PARTS):
            for k in range(1, TEAM):
                out_copy(s, mate(k), part, j).wait_send()
                out_copy(s, j, part, mate(k)).wait_recv()
            out_local(s, part).wait()


def fused(ng, ny, q, k, v, block_list, block_count):
    anywhere = pl.BlockSpec(memory_space=pl.ANY)
    buf = pltpu.VMEM((ng * 2 * TEAM, 2, BLK, D), jnp.bfloat16)
    dma = pltpu.SemaphoreType.DMA
    return pl.pallas_call(
        functools.partial(kernel, ng, ny),
        in_specs=[anywhere] * 5,
        out_specs=anywhere,
        out_shape=jax.ShapeDtypeStruct(q.shape, jnp.bfloat16),
        scratch_shapes=[
            buf,
            buf,
            pltpu.VMEM((KVH, 2, BLK, D), jnp.bfloat16),
            pltpu.VMEM((STAGES, TEAM, BLK, COLS), jnp.bfloat16),
            pltpu.VMEM((STAGES, TEAM, BLK, COLS), jnp.bfloat16),
            pltpu.VMEM((2, 2, MAXB * BLK, BLK), jnp.float32),
            pltpu.VMEM((BLK, KVH * D), jnp.bfloat16),
            pltpu.VMEM((BLK, KVH * D), jnp.bfloat16),
            pltpu.SMEM((2 * TEAM, MAXB, H), jnp.int32),
            pltpu.SMEM((2 * TEAM, H), jnp.int32),
            dma((2,)),
            dma((2,)),
            dma((STAGES,)),
            dma((STAGES, PARTS)),
            dma((STAGES, TEAM)),
            dma((STAGES, TEAM)),
            dma((STAGES, TEAM)),
            dma((STAGES, TEAM, PARTS)),
            dma((STAGES, TEAM, PARTS)),
            dma((STAGES, ng, TEAM)),
            dma((STAGES, ng, TEAM)),
            dma((STAGES, ng, TEAM)),
            dma((STAGES, ng, TEAM)),
        ],
        compiler_params=pltpu.CompilerParams(
            collective_id=0, has_side_effects=True, vmem_limit_bytes=48 * 1024 * 1024
        ),
        name="heads_attend",
    )(*(pltpu.with_memory_space_constraint(x, pltpu.HBM) for x in (q, k, v, block_list, block_count)))


def shards(q, k, v, block_list, block_count):
    ny = lax.axis_size("y")
    ng = lax.axis_size("seq") * ny // TEAM
    return fused(ng, ny, q, k, v, block_list.transpose(1, 2, 0), block_count.T)


def solution(mesh):
    n_seq, n_qblk = mesh.devices.shape
    fine = Mesh(mesh.devices.reshape(n_seq, n_qblk // 2, 2), ("seq", "y", "core"))
    rows = P(("seq", "y", "core"), None)
    return jax.shard_map(
        shards,
        mesh=fine,
        in_specs=(rows, rows, rows, P(), P()),
        out_specs=rows,
        check_vma=False,
    )
```
